128 devices in a mesh: fsdp: 32 (over y, x_lo, z), tp: 4 (over x_hi, core).
Axes of the slice: x: 4 (x_hi: 2, x_lo: 2; x = x_hi * 2 + x_lo), y: 4, z: 4, core: 2. Of those that a mesh axis runs over, the one named last changes fastest.
Arguments:
- inputs: bfloat16 [8192, 1024], P('fsdp'), may hold values from -6 to 6
- out_grads: bfloat16 [8192, 24, 1024], P('fsdp', None, 'tp'), may hold values from -0.0625 to 0.0625
- momentum: float32 [1024, 24, 1024], P('fsdp', None, 'tp'), may hold values from -6 to 6
Outputs:
- new_momentum: float32 [1024, 24, 1024], P('fsdp', None, 'tp')
- update: float32 [1024, 24, 1024], P('fsdp', None, 'tp')
The draws below stay inside these ranges and needn't reach their ends.
All inputs are finite; a program needn't handle non-finite values.
Results may differ from the reference program's by a relative error of at most 0.01.
Values may be sent and summed in bfloat16 or wider, within the bound.
A program may use at most 128 MiB of HBM per device.

```python
import math
import jax
import jax.numpy as jnp

D = 1024
NMAT = 24
ITERS = 2
TOKENS = 8192


def spiked(result, key, source, target, parts, factor):
    def block_of(position):
        return (jnp.arange(result.shape[position]) // (result.shape[position] // parts)).reshape((-1,) + (1,) * (result.ndim - 1 - position))

    one_side = jax.random.permutation(key, parts)[block_of(target)]
    second = (block_of(target) + parts // 2) % parts
    return jnp.where((block_of(source) == one_side) | (block_of(source) == second), factor * result, result)


def block_scale(key, dims, pieces, low, top_value):
    gain = 1.0
    for position, parts in pieces:
        draws = jax.random.uniform(jax.random.fold_in(jax.random.fold_in(key, 6), position), (parts,), jnp.float32, low / len(pieces), top_value / len(pieces))
        gain = gain * jnp.repeat(jnp.exp(draws), dims[position] // parts).reshape((-1,) + (1,) * (len(dims) - 1 - position))
    return gain


def scatter_about(own_key, dims, deviation, limit, split=(), dtype=jnp.bfloat16):
    gain = block_scale(own_key, dims, split, -0.22, 0.18) if split else 1.0
    values = jax.random.normal(own_key, dims, jnp.float32) * deviation * gain
    return jnp.minimum(jnp.maximum(values, -limit), limit).astype(dtype)


def bell_draw_with(own_key, extent, scale, most, shards, heavy, held_as=jnp.bfloat16):
    array = scale * jax.random.normal(own_key, extent, jnp.float32)
    if shards:
        array = array * block_scale(own_key, extent, shards, -0.22, 0.18)
    return jnp.clip(spiked(array, jax.random.fold_in(own_key, 3), *heavy), -most, most).astype(held_as)


def setup_inputs(seed: int = 0) -> dict:
    splits = jax.random.split(jax.random.key(seed), 4)
    inputs = bell_draw_with(splits[0], (TOKENS, D), 1.0, 6.0, ((0, 32),), (0, 1, 32, 2.75))
    out_grads = scatter_about(splits[1], (TOKENS, NMAT, D), (TOKENS ** -0.5), 0.0625, ((0, 32), (2, 4)))
    momentum = scatter_about(splits[2], (D, NMAT, D), 1.0, 6.0, ((0, 32), (2, 4)), jnp.float32)
    return dict(inputs=inputs, out_grads=out_grads, momentum=momentum)


def reference(inputs, out_grads, momentum):
    width = inputs.shape[1]
    news = []
    steps = []
    for index in range(NMAT):
        grad = jnp.dot(inputs.T, out_grads[:, index, :], preferred_element_type=jnp.float32)
        moment = 0.95 * momentum[:, index, :] + grad
        nesterov = (grad + 0.95 * moment).astype(jnp.bfloat16)
        widened = nesterov.astype(jnp.float32)
        scale = jnp.sqrt(jnp.sum(widened * widened)) + 1e-07
        current = (widened / scale).astype(jnp.bfloat16)
        for turn in range(ITERS):
            gram = jnp.dot(current, current.T, preferred_element_type=jnp.float32).astype(jnp.bfloat16)
            square = jnp.dot(gram, gram, preferred_element_type=jnp.float32)
            mixer = (-4.775 * gram.astype(jnp.float32) + 2.0315 * square).astype(jnp.bfloat16)
            current = (3.4445 * current.astype(jnp.float32) + jnp.dot(mixer, current, preferred_element_type=jnp.float32)).astype(jnp.bfloat16)
        news.append(moment)
        steps.append(current.astype(jnp.float32) * (0.2 * math.sqrt(width)))
    return (jnp.stack(news, axis=1), jnp.stack(steps, axis=1))
```

```python
import functools
import math

import jax
import jax.numpy as jnp
from jax import lax
from jax.experimental import pallas as pl
from jax.experimental.pallas import tpu as pltpu
from jax.sharding import PartitionSpec as P

ITERS = 2
NZ = 4
MESH = pl.DeviceIdType.MESH
F32 = jnp.float32
BF16 = jnp.bfloat16


def landed(ref, sem):
    pltpu.make_async_copy(ref, ref, sem).wait()


def gather_kernel(
    planes, xt_ref, og_ref, mom_ref, home_ref, full_ref,
    xall, ogs, moms, part, sums, gbuf, nbuf, full, home,
    x_s, x_r, f_s, f_r, og_s, og_r, mo_s, mo_r, rs_s, rs_r, n_s, n_r, nf_s, nf_r, h_s, h_r, loc,
):
    fs = lax.axis_index("fsdp")
    t = lax.axis_index("tp")
    p, z = fs // NZ, fs % NZ
    xh, c = t // 2, t % 2
    partner = xh * 2 + (1 - c)
    each = ogs.shape[0]
    tok = og_ref.shape[1]
    cols = og_ref.shape[2]
    rows = xall.shape[0]
    half = rows // 2
    block = rows // planes
    piece = block // NZ

    barrier = pltpu.get_barrier_semaphore()

    def greet(f, tp):
        pl.semaphore_signal(barrier, inc=1, device_id=(f, tp), device_id_type=MESH)

    for d in range(1, NZ):
        greet(p * NZ + (z + d) % NZ, t)
    for d in range(1, planes):
        for other in range(2):
            greet((p + d) % planes * NZ + z, other * 2 + c)
    greet(fs, (1 - xh) * 2 + c)
    greet(fs, partner)
    pl.semaphore_wait(barrier, NZ - 1 + 2 * (planes - 1) + 2)

    def x_view(slot, side):
        return xall.at[pl.ds(pl.multiple_of(side * half, half), half), pl.ds(pl.multiple_of(slot * tok, tok), tok)]

    def x_copy(d):
        return pltpu.make_async_remote_copy(
            xt_ref.at[pl.ds(pl.multiple_of(c * half, half), half), :], x_view(z, c), x_s.at[d], x_r.at[z],
            device_id=(p * NZ + (z + d) % NZ, t), device_id_type=MESH)

    def x_forward(slot):
        return pltpu.make_async_remote_copy(
            x_view(slot, c), x_view(slot, c), f_s.at[slot], f_r.at[slot],
            device_id=(fs, partner), device_id_type=MESH)

    def og_view(slot, k):
        return ogs.at[k, pl.ds(pl.multiple_of(slot * tok, tok), tok), :]

    def og_copy(d, k):
        to = (z + d) % NZ
        return pltpu.make_async_remote_copy(
            og_ref.at[to * each + k], og_view(z, k), og_s.at[k, d], og_r.at[k, z],
            device_id=(p * NZ + to, t), device_id_type=MESH)

    def mom_copy(d):
        to = (z + d) % NZ
        return pltpu.make_async_remote_copy(
            mom_ref.at[pl.ds(to * each, each)], moms.at[z], mo_s.at[d], mo_r.at[z],
            device_id=(p * NZ + to, t), device_id_type=MESH)

    own_x = pltpu.make_async_copy(xt_ref, xall.at[:, pl.ds(pl.multiple_of(z * tok, tok), tok)], loc.at[0])
    own_og = pltpu.make_async_copy(
        og_ref.at[pl.ds(z * each, each)], ogs.at[:, pl.ds(pl.multiple_of(z * tok, tok), tok), :], loc.at[1])
    own_mom = pltpu.make_async_copy(mom_ref.at[pl.ds(z * each, each)], moms.at[z], loc.at[2])

    for d in (2, 1, 3):
        x_copy(d).start()

    @pl.loop(0, each)
    def _(k):
        for d in (2, 1, 3):
            og_copy(d, k).start()

    for d in (2, 1, 3):
        mom_copy(d).start()
    own_x.start()
    own_og.start()
    own_mom.start()

    for d in (1, 3, 2):
        slot = (z + d) % NZ
        landed(x_view(slot, c), x_r.at[slot])
        x_forward(slot).start()
    own_x.wait()
    own_og.wait()
    own_mom.wait()
    for d in (1, 3, 2):
        slot = (z + d) % NZ
        landed(x_view(slot, 1 - c), f_r.at[slot])

    def rs_copy(k, to):
        return pltpu.make_async_remote_copy(
            part.at[k, to], sums.at[k, p], rs_s.at[k, to], rs_r.at[k, p],
            device_id=(to * NZ + z, t), device_id_type=MESH)

    def full_view(at, col):
        return full.at[pl.ds(pl.multiple_of(at * block, block), block), pl.ds(pl.multiple_of(col * cols, cols), cols)]

    def n_copy(k, other):
        return pltpu.make_async_remote_copy(
            nbuf.at[k], full_view(p, t), n_s.at[k, other], n_r.at[p, xh],
            device_id=(k * NZ + z, other * 2 + c), device_id_type=MESH)

    def n_local(k):
        return pltpu.make_async_copy(nbuf.at[k], full_view(p, t), n_r.at[p, xh])

    def multiply(k):
        for d in range(1, NZ):
            slot = (z + d) % NZ
            landed(og_view(slot, k), og_r.at[k, slot])
        step = 2 * block
        for r in range(planes // 2):
            acc = jnp.dot(xall[r * step:(r + 1) * step, :], ogs[k], preferred_element_type=F32)
            part[k, 2 * r] = acc[:block].astype(BF16)
            part[k, 2 * r + 1] = acc[block:].astype(BF16)
            for to in (2 * r, 2 * r + 1):
                @pl.when(p != to)
                def _():
                    rs_copy(k, to).start()

    def combine(k):
        total = part[k, p].astype(F32)
        for d in range(1, planes):
            source = (p + d) % planes
            landed(sums.at[k, source], rs_r.at[k, source])
            total = total + sums[k, source].astype(F32)
        momentum = moms[:, k].reshape(block, cols).astype(F32)
        gbuf[k] = total.astype(BF16)
        nbuf[k] = (total + 0.95 * (0.95 * momentum + total)).astype(BF16)
        for other in range(2):
            mine = jnp.logical_and(k == p, xh == other)

            @pl.when(jnp.logical_not(mine))
            def _():
                n_copy(k, other).start()

            @pl.when(mine)
            def _():
                n_local(k).start()

    multiply(0)
    for d in (1, 2, 3):
        slot = (z + d) % NZ
        landed(moms.at[slot], mo_r.at[slot])

    @pl.loop(1, each)
    def _(k):
        multiply(k)
        combine(k - 1)

    combine(each - 1)

    def home_copy(d):
        to = (z + d) % NZ
        return pltpu.make_async_remote_copy(
            gbuf.at[:, pl.ds(pl.multiple_of(to * piece, piece), piece), :], home.at[pl.ds(z * each, each)],
            h_s.at[d], h_r.at[z], device_id=(p * NZ + to, t), device_id_type=MESH)

    for d in range(1, NZ):
        home_copy(d).start()
    own_home = pltpu.make_async_copy(
        gbuf.at[:, pl.ds(pl.multiple_of(z * piece, piece), piece), :], home.at[pl.ds(z * each, each)], loc.at[3])
    own_home.start()

    def n_forward(at, other):
        return pltpu.make_async_remote_copy(
            full_view(at, other * 2 + c), full_view(at, other * 2 + c), nf_s.at[at, other], nf_r.at[at, other],
            device_id=(fs, partner), device_id_type=MESH)

    @pl.when(p < each)
    def _():
        @pl.loop(0, planes)
        def _(at):
            for other in range(2):
                landed(full_view(at, other * 2 + c), n_r.at[at, other])
                n_forward(at, other).start()

        @pl.loop(0, planes)
        def _(at):
            for other in range(2):
                landed(full_view(at, other * 2 + 1 - c), nf_r.at[at, other])
                n_forward(at, other).wait_send()

    full_ref[...] = full[...]
    own_home.wait()
    for d in range(1, NZ):
        slot = (z + d) % NZ
        landed(home.at[pl.ds(slot * each, each)], h_r.at[slot])
    home_ref[...] = home[...]

    for d in range(1, NZ):
        x_copy(d).wait_send()
        x_forward((z + d) % NZ).wait_send()
        mom_copy(d).wait_send()
        home_copy(d).wait_send()

    @pl.loop(0, each)
    def _(k):
        for d in range(1, NZ):
            og_copy(d, k).wait_send()
        for d in range(1, planes):
            rs_copy(k, (p + d) % planes).wait_send()
        for other in range(2):
            @pl.when(jnp.logical_not(jnp.logical_and(k == p, xh == other)))
            def _():
                n_copy(k, other).wait_send()


def newton_kernel(x_ref, out_ref, xs, gram, mix):
    rows = x_ref.shape[0]
    cols = out_ref.shape[1]
    step = 256
    start = pl.multiple_of(lax.axis_index("tp") * cols, cols)
    acc = jnp.zeros((step, rows), F32)
    for r in range(0, rows, step):
        wide = x_ref[r:r + step, :].astype(F32)
        acc = acc + wide * wide
    scale = jnp.sqrt(jnp.sum(acc)) + 1e-07
    inverse = 1.0 / scale
    for r in range(0, rows, step):
        xs[0, r:r + step, :] = (x_ref[r:r + step, :].astype(F32) * inverse).astype(BF16)
    for turn in range(ITERS):
        x = xs.at[turn]

        @pl.loop(0, rows, step=step)
        def _(r):
            here = pl.ds(pl.multiple_of(r, step), step)
            gram[here, :] = lax.dot_general(
                x[here, :], x[...], (((1,), (1,)), ((), ())), preferred_element_type=F32).astype(BF16)

        @pl.loop(0, rows, step=step)
        def _(r):
            here = pl.ds(pl.multiple_of(r, step), step)
            square = jnp.dot(gram[here, :], gram[...], preferred_element_type=F32)
            mix[here, :] = (-4.775 * gram[here, :].astype(F32) + 2.0315 * square).astype(BF16)

        @pl.loop(0, rows, step=step)
        def _(r):
            here = pl.ds(pl.multiple_of(r, step), step)
            wanted = pl.ds(start, cols) if turn == ITERS - 1 else slice(None)
            product = jnp.dot(mix[here, :], x[:, wanted], preferred_element_type=F32)
            result = (3.4445 * x[here, wanted].astype(F32) + product).astype(BF16)
            if turn == ITERS - 1:
                out_ref[here, :] = result
            else:
                xs[turn + 1, here, :] = result


def return_kernel(planes, groups, each, final_ref, out_ref, back, send, recv, loc):
    fs = lax.axis_index("fsdp")
    t = lax.axis_index("tp")
    p, z = fs // NZ, fs % NZ
    piece = back.shape[1]
    barrier = pltpu.get_barrier_semaphore()

    @pl.loop(1, groups)
    def _(d):
        pl.semaphore_signal(barrier, inc=1, device_id=((fs + d) % groups, t), device_id_type=MESH)

    pl.semaphore_wait(barrier, groups - 1)
    matrix = z * each + p

    def copy(to):
        return pltpu.make_async_remote_copy(
            final_ref.at[pl.ds(pl.multiple_of(to * piece, piece), piece), :], back.at[matrix], send.at[to],
            recv.at[matrix], device_id=(to, t), device_id_type=MESH)

    own = pltpu.make_async_copy(
        final_ref.at[pl.ds(pl.multiple_of(fs * piece, piece), piece), :], back.at[matrix], loc)

    @pl.when(p < each)
    def _():
        @pl.loop(1, groups)
        def _(d):
            copy((fs + d) % groups).start()

        own.start()
        own.wait()

    @pl.loop(0, groups)
    def _(source):
        sp, sz = source // NZ, source % NZ

        @pl.when(jnp.logical_and(sp < each, source != fs))
        def _():
            landed(back.at[sz * each + sp], recv.at[sz * each + sp])

    out_ref[...] = back[...]

    @pl.when(p < each)
    def _():
        @pl.loop(1, groups)
        def _(d):
            copy((fs + d) % groups).wait_send()


def local(inputs, out_grads, momentum):
    groups = lax.axis_size("fsdp")
    planes = groups // NZ
    tok, count, cols = out_grads.shape
    rows = inputs.shape[1]
    piece = momentum.shape[0]
    each = count // NZ
    block = rows // planes
    dma = pltpu.SemaphoreType.DMA
    vmem = pl.BlockSpec(memory_space=pltpu.VMEM)
    hbm = pl.BlockSpec(memory_space=pl.ANY)

    xt = inputs.T
    og = out_grads.transpose(1, 0, 2)
    mom = momentum.transpose(1, 0, 2).astype(BF16)
    home, full = pl.pallas_call(
        functools.partial(gather_kernel, planes),
        out_shape=(jax.ShapeDtypeStruct((count, piece, cols), BF16), jax.ShapeDtypeStruct((rows, rows), BF16)),
        in_specs=[hbm, hbm, hbm],
        out_specs=(vmem, vmem),
        scratch_shapes=[
            pltpu.VMEM((rows, NZ * tok), BF16),
            pltpu.VMEM((each, NZ * tok, cols), BF16),
            pltpu.VMEM((NZ, each, piece, cols), BF16),
            pltpu.VMEM((each, planes, block, cols), BF16),
            pltpu.VMEM((each, planes, block, cols), BF16),
            pltpu.VMEM((each, block, cols), BF16),
            pltpu.VMEM((each, block, cols), BF16),
            pltpu.VMEM((rows, rows), BF16),
            pltpu.VMEM((count, piece, cols), BF16),
            dma((NZ,)), dma((NZ,)), dma((NZ,)), dma((NZ,)),
            dma((each, NZ)), dma((each, NZ)), dma((NZ,)), dma((NZ,)),
            dma((each, planes)), dma((each, planes)),
            dma((each, 2)), dma((planes, 2)), dma((planes, 2)), dma((planes, 2)),
            dma((NZ,)), dma((NZ,)), dma((4,)),
        ],
        compiler_params=pltpu.CompilerParams(
            collective_id=0, has_side_effects=True, vmem_limit_bytes=48 * 1024 * 1024),
        name="gather",
    )(xt, og, mom)
    final = pl.pallas_call(
        newton_kernel,
        out_shape=jax.ShapeDtypeStruct((rows, cols), BF16),
        in_specs=[vmem],
        out_specs=vmem,
        scratch_shapes=[
            pltpu.VMEM((ITERS, rows, rows), BF16),
            pltpu.VMEM((rows, rows), BF16),
            pltpu.VMEM((rows, rows), BF16),
        ],
        compiler_params=pltpu.CompilerParams(vmem_limit_bytes=48 * 1024 * 1024),
        name="newton",
    )(full)
    back = pl.pallas_call(
        functools.partial(return_kernel, planes, groups, each),
        out_shape=jax.ShapeDtypeStruct((count, piece, cols), BF16),
        in_specs=[vmem],
        out_specs=vmem,
        scratch_shapes=[
            pltpu.VMEM((count, piece, cols), BF16),
            dma((groups,)), dma((count,)), dma,
        ],
        compiler_params=pltpu.CompilerParams(collective_id=1, has_side_effects=True),
        name="give_back",
    )(final)
    new_momentum = 0.95 * momentum + home.transpose(1, 0, 2).astype(F32)
    update = back.transpose(1, 0, 2).astype(F32) * (0.2 * math.sqrt(rows))
    return (new_momentum, update)


def solution(mesh):
    in_specs = (P("fsdp", None), P("fsdp", None, "tp"), P("fsdp", None, "tp"))
    out_specs = (P("fsdp", None, "tp"), P("fsdp", None, "tp"))
    return jax.shard_map(local, mesh=mesh, in_specs=in_specs, out_specs=out_specs, check_vma=False)
```

```python
import functools
import math

import jax
import jax.numpy as jnp
from jax import lax
from jax.experimental import pallas as pl
from jax.experimental.pallas import tpu as pltpu
from jax.sharding import PartitionSpec as P

ITERS = 2
NZ = 4
MESH = pl.DeviceIdType.MESH
F32 = jnp.float32
BF16 = jnp.bfloat16


def landed(ref, sem):
    pltpu.make_async_copy(ref, ref, sem).wait()


def step_kernel(
    groups, x_ref, grads_ref, momentum_ref, home, back,
    xt_ref, og_ref, mom_ref, xall, ogs, moms, part, sums, gbuf, nbuf, full, xs, gram, mix, final,
    x_s, x_r, f_s, f_r, og_s, og_r, mo_s, mo_r, rs_s, rs_r, n_s, n_r, nf_s, nf_r, h_s, h_r, b_s, b_r, loc,
):
    planes = groups // NZ
    fs = lax.axis_index("fsdp")
    t = lax.axis_index("tp")
    p, z = fs // NZ, fs % NZ
    xh, c = t // 2, t % 2
    partner = xh * 2 + (1 - c)
    each = ogs.shape[0]
    tok = og_ref.shape[1]
    cols = og_ref.shape[2]
    rows = xall.shape[0]
    half = rows // 2
    block = rows // planes
    piece = block // NZ
    pairs = each // 2
    lanes = cols // 2

    barrier = pltpu.get_barrier_semaphore()

    def greet(f, tp):
        pl.semaphore_signal(barrier, inc=1, device_id=(f, tp), device_id_type=MESH)

    @pl.loop(1, groups)
    def _(d):
        greet((fs + d) % groups, t)

    @pl.loop(0, planes)
    def _(at):
        greet(at * NZ + z, (1 - xh) * 2 + c)

    greet(fs, partner)
    xt_ref[...] = x_ref[...].T

    def places():
        for m in range(NZ * each):
            for h in range(2):
                low = m % each
                yield m, h, m - low + h * pairs + low // 2, low % 2 * lanes

    @pl.loop(0, tok, step=16)
    def _(at):
        here = pl.ds(pl.multiple_of(at, 16), 16)
        turned = jnp.swapaxes(grads_ref[here].astype(F32), 0, 1).astype(BF16)
        for m, h, to, lane in places():
            og_ref[to, here, lane:lane + lanes] = turned[m, :, h * lanes:(h + 1) * lanes]

    turned = jnp.swapaxes(momentum_ref[...], 0, 1).astype(BF16)
    for m, h, to, lane in places():
        mom_ref[to, :, lane:lane + lanes] = turned[m, :, h * lanes:(h + 1) * lanes]
    pl.semaphore_wait(barrier, groups + planes)

    def x_view(slot, side):
        return xall.at[pl.ds(pl.multiple_of(side * half, half), half), pl.ds(pl.multiple_of(slot * tok, tok), tok)]

    def x_copy(d):
        return pltpu.make_async_remote_copy(
            xt_ref.at[pl.ds(pl.multiple_of(c * half, half), half), :], x_view(z, c), x_s.at[d], x_r.at[z],
            device_id=(p * NZ + (z + d) % NZ, t), device_id_type=MESH)

    def x_forward(slot):
        return pltpu.make_async_remote_copy(
            x_view(slot, c), x_view(slot, c), f_s.at[slot], f_r.at[slot],
            device_id=(fs, partner), device_id_type=MESH)

    def og_view(slot, k):
        return ogs.at[k, pl.ds(pl.multiple_of(slot * tok, tok), tok), :]

    def og_copy(d, k):
        to = (z + d) % NZ
        return pltpu.make_async_remote_copy(
            og_ref.at[to * each + k], og_view(z, k), og_s.at[k, d], og_r.at[k, z],
            device_id=(p * NZ + to, t), device_id_type=MESH)

    def mom_copy(d, k):
        to = (z + d) % NZ
        return pltpu.make_async_remote_copy(
            mom_ref.at[to * each + k], moms.at[z, k], mo_s.at[k, d], mo_r.at[k, z],
            device_id=(p * NZ + to, t), device_id_type=MESH)

    own_x = pltpu.make_async_copy(xt_ref, xall.at[:, pl.ds(pl.multiple_of(z * tok, tok), tok)], loc.at[0])
    own_og = pltpu.make_async_copy(
        og_ref.at[pl.ds(z * each, each)], ogs.at[:, pl.ds(pl.multiple_of(z * tok, tok), tok), :], loc.at[1])
    own_mom = pltpu.make_async_copy(mom_ref.at[pl.ds(z * each, each)], moms.at[z], loc.at[2])

    for d in (2, 1, 3):
        x_copy(d).start()

    @pl.loop(0, each)
    def _(k):
        for d in (2, 1, 3):
            og_copy(d, k).start()
        for d in (2, 1, 3):
            mom_copy(d, k).start()

    own_x.start()
    own_og.start()
    own_mom.start()

    for d in (1, 3, 2):
        slot = (z + d) % NZ
        landed(x_view(slot, c), x_r.at[slot])
        x_forward(slot).start()
    own_x.wait()
    own_og.wait()
    own_mom.wait()
    for d in (1, 3, 2):
        slot = (z + d) % NZ
        landed(x_view(slot, 1 - c), f_r.at[slot])

    def rs_copy(k, to):
        return pltpu.make_async_remote_copy(
            part.at[k, to], sums.at[k, p], rs_s.at[k, to], rs_r.at[k, p],
            device_id=(to * NZ + z, t), device_id_type=MESH)

    def half_view(at, col, h):
        return full.at[
            pl.ds(pl.multiple_of(at * block, block), block), pl.ds(pl.multiple_of(col * cols + h * lanes, lanes), lanes)]

    def n_copy(k, mm, other):
        h, pair = k // pairs, k % pairs
        return pltpu.make_async_remote_copy(
            nbuf.at[k, :, mm * lanes:(mm + 1) * lanes], half_view(p, t, h), n_s.at[k, mm, other], n_r.at[h, p, xh],
            device_id=((pair * 2 + mm) * NZ + z, other * 2 + c), device_id_type=MESH)

    def n_local(k, mm):
        h = k // pairs
        return pltpu.make_async_copy(nbuf.at[k, :, mm * lanes:(mm + 1) * lanes], half_view(p, t, h), n_r.at[h, p, xh])

    def n_mine(k, mm, other):
        return jnp.logical_and(k % pairs * 2 + mm == p, xh == other)

    def multiply(k):
        for d in range(1, NZ):
            slot = (z + d) % NZ
            landed(og_view(slot, k), og_r.at[k, slot])
        step = 2 * block
        for r in range(planes // 2):
            acc = jnp.dot(xall[r * step:(r + 1) * step, :], ogs[k], preferred_element_type=F32)
            part[k, 2 * r] = acc[:block].astype(BF16)
            part[k, 2 * r + 1] = acc[block:].astype(BF16)
            for to in (2 * r, 2 * r + 1):
                @pl.when(p != to)
                def _():
                    rs_copy(k, to).start()

    def combine(k):
        total = part[k, p].astype(F32)
        for d in range(1, planes):
            source = (p + d) % planes
            landed(sums.at[k, source], rs_r.at[k, source])
            total = total + sums[k, source].astype(F32)
        for d in range(1, NZ):
            slot = (z + d) % NZ
            landed(moms.at[slot, k], mo_r.at[k, slot])
        momentum = moms[:, k].reshape(block, cols).astype(F32)
        gbuf[k] = total.astype(BF16)
        nbuf[k] = (total + 0.95 * (0.95 * momentum + total)).astype(BF16)
        for mm in range(2):
            for other in range(2):
                mine = n_mine(k, mm, other)

                @pl.when(jnp.logical_not(mine))
                def _():
                    n_copy(k, mm, other).start()

                @pl.when(mine)
                def _():
                    n_local(k, mm).start()

    multiply(0)
    @pl.loop(1, each)
    def _(k):
        multiply(k)
        combine(k - 1)

    combine(each - 1)

    def home_copy(d):
        to = (z + d) % NZ
        return pltpu.make_async_remote_copy(
            gbuf.at[:, pl.ds(pl.multiple_of(to * piece, piece), piece), :], home.at[pl.ds(z * each, each)],
            h_s.at[d], h_r.at[z], device_id=(p * NZ + to, t), device_id_type=MESH)

    for d in range(1, NZ):
        home_copy(d).start()
    own_home = pltpu.make_async_copy(
        gbuf.at[:, pl.ds(pl.multiple_of(z * piece, piece), piece), :], home.at[pl.ds(z * each, each)], loc.at[3])
    own_home.start()

    def n_forward(h, at, other):
        view = half_view(at, other * 2 + c, h)
        return pltpu.make_async_remote_copy(
            view, view, nf_s.at[h, at, other], nf_r.at[h, at, other],
            device_id=(fs, partner), device_id_type=MESH)

    matrix = z * each + p

    def back_copy(to):
        return pltpu.make_async_remote_copy(
            final.at[pl.ds(pl.multiple_of(to * piece, piece), piece), :], back.at[matrix], b_s.at[to],
            b_r.at[matrix], device_id=(to, t), device_id_type=MESH)

    def newton():
        step = 256
        homes = step // piece
        wanted = pl.ds(pl.multiple_of(t * cols, cols), cols)
        acc = jnp.zeros((step, rows), F32)
        for r in range(0, rows, step):
            wide = full[r:r + step, :].astype(F32)
            acc = acc + wide * wide
        scale = jnp.sqrt(jnp.sum(acc)) + 1e-07
        inverse = 1.0 / scale
        for r in range(0, rows, step):
            xs[0, r:r + step, :] = (full[r:r + step, :].astype(F32) * inverse).astype(BF16)
        for turn in range(ITERS):
            x = xs.at[turn]

            @pl.loop(0, rows, step=step)
            def _(r):
                here = pl.ds(pl.multiple_of(r, step), step)
                gram[here, :] = lax.dot_general(
                    x[here, :], x[...], (((1,), (1,)), ((), ())), preferred_element_type=F32).astype(BF16)

            @pl.loop(0, rows, step=step)
            def _(r):
                here = pl.ds(pl.multiple_of(r, step), step)
                square = jnp.dot(gram[here, :], gram[...], preferred_element_type=F32)
                mix[here, :] = (-4.775 * gram[here, :].astype(F32) + 2.0315 * square).astype(BF16)

            @pl.loop(0, rows // step)
            def _(i):
                if turn < ITERS - 1:
                    here = pl.ds(pl.multiple_of(i * step, step), step)
                    product = jnp.dot(mix[here, :], x[...], preferred_element_type=F32)
                    xs[turn + 1, here, :] = (3.4445 * x[here, :].astype(F32) + product).astype(BF16)
                else:
                    part_at = (i + p) % (rows // step)
                    here = pl.ds(pl.multiple_of(part_at * step, step), step)
                    product = jnp.dot(mix[here, :], x[:, wanted], preferred_element_type=F32)
                    final[here, :] = (3.4445 * x[here, wanted].astype(F32) + product).astype(BF16)

                    @pl.loop(0, homes)
                    def _(h):
                        to = part_at * homes + (h + z) % homes

                        @pl.when(to != fs)
                        def _():
                            back_copy(to).start()

        own = pltpu.make_async_copy(
            final.at[pl.ds(pl.multiple_of(fs * piece, piece), piece), :], back.at[matrix], b_r.at[matrix])
        own.start()

    @pl.when(p < each)
    def _():
        for h in range(2):
            @pl.loop(0, planes)
            def _(step):
                at = (p + step) % planes
                for other in range(2):
                    landed(half_view(at, other * 2 + c, h), n_r.at[h, at, other])
                    n_forward(h, at, other).start()

        for h in range(2):
            @pl.loop(0, planes)
            def _(step):
                at = (p + step) % planes
                for other in range(2):
                    landed(half_view(at, other * 2 + 1 - c, h), nf_r.at[h, at, other])
                    n_forward(h, at, other).wait_send()

        newton()

    own_home.wait()
    for d in range(1, NZ):
        slot = (z + d) % NZ
        landed(home.at[pl.ds(slot * each, each)], h_r.at[slot])

    @pl.loop(0, groups)
    def _(source):
        sp, sz = source // NZ, source % NZ

        @pl.when(sp < each)
        def _():
            landed(back.at[sz * each + sp], b_r.at[sz * each + sp])

    @pl.when(p < each)
    def _():
        @pl.loop(1, groups)
        def _(d):
            back_copy((fs + d) % groups).wait_send()

    for d in range(1, NZ):
        x_copy(d).wait_send()
        x_forward((z + d) % NZ).wait_send()
        home_copy(d).wait_send()

    @pl.loop(0, each)
    def _(k):
        for d in range(1, NZ):
            og_copy(d, k).wait_send()
            mom_copy(d, k).wait_send()
        for d in range(1, planes):
            rs_copy(k, (p + d) % planes).wait_send()
        for mm in range(2):
            for other in range(2):
                @pl.when(jnp.logical_not(n_mine(k, mm, other)))
                def _():
                    n_copy(k, mm, other).wait_send()


def finish_kernel(each, rows, home, back, momentum_ref, new_ref, update_ref):
    count, piece, cols = home.shape
    pairs = each // 2
    lanes = cols // 2

    def grad(m, h):
        low = m % each
        lane = low % 2 * lanes
        return home[m - low + h * pairs + low // 2, :, lane:lane + lanes]

    for base in range(0, count, 8):
        group = slice(base, base + 8)
        update_ref[:, group, :] = jnp.swapaxes(back[group].astype(F32), 0, 1) * (0.2 * math.sqrt(rows))
        for h in range(2):
            here = slice(h * lanes, (h + 1) * lanes)
            grads = jnp.stack([grad(m, h) for m in range(base, base + 8)]).astype(F32)
            new_ref[:, group, here] = 0.95 * momentum_ref[:, group, here] + jnp.swapaxes(grads, 0, 1)


def local(inputs, out_grads, momentum):
    groups = lax.axis_size("fsdp")
    planes = groups // NZ
    tok, count, cols = out_grads.shape
    rows = inputs.shape[1]
    piece = momentum.shape[0]
    each = count // NZ
    block = rows // planes
    dma = pltpu.SemaphoreType.DMA
    vmem = pl.BlockSpec(memory_space=pltpu.VMEM)
    hbm = pl.BlockSpec(memory_space=pl.ANY)

    small = jax.ShapeDtypeStruct((count, piece, cols), BF16)
    home, back = pl.pallas_call(
        functools.partial(step_kernel, groups),
        out_shape=(small, small),
        in_specs=[vmem, vmem, vmem],
        out_specs=(hbm, hbm),
        scratch_shapes=[
            pltpu.VMEM((rows, tok), BF16),
            pltpu.VMEM((count, tok, cols), BF16),
            pltpu.VMEM((count, piece, cols), BF16),
            pltpu.VMEM((rows, NZ * tok), BF16),
            pltpu.VMEM((each, NZ * tok, cols), BF16),
            pltpu.VMEM((NZ, each, piece, cols), BF16),
            pltpu.VMEM((each, planes, block, cols), BF16),
            pltpu.VMEM((each, planes, block, cols), BF16),
            pltpu.VMEM((each, block, cols), BF16),
            pltpu.VMEM((each, block, cols), BF16),
            pltpu.VMEM((rows, rows), BF16),
            pltpu.VMEM((ITERS, rows, rows), BF16),
            pltpu.VMEM((rows, rows), BF16),
            pltpu.VMEM((rows, rows), BF16),
            pltpu.VMEM((rows, cols), BF16),
            dma((NZ,)), dma((NZ,)), dma((NZ,)), dma((NZ,)),
            dma((each, NZ)), dma((each, NZ)), dma((each, NZ)), dma((each, NZ)),
            dma((each, planes)), dma((each, planes)),
            dma((each, 2, 2)), dma((2, planes, 2)), dma((2, planes, 2)), dma((2, planes, 2)),
            dma((NZ,)), dma((NZ,)), dma((groups,)), dma((count,)), dma((4,)),
        ],
        compiler_params=pltpu.CompilerParams(
            collective_id=0, has_side_effects=True, vmem_limit_bytes=56 * 1024 * 1024),
        name="muon_step",
    )(inputs, out_grads, momentum)
    return pl.pallas_call(
        functools.partial(finish_kernel, each, rows),
        out_shape=(jax.ShapeDtypeStruct(momentum.shape, F32), jax.ShapeDtypeStruct(momentum.shape, F32)),
        in_specs=[vmem, vmem, vmem],
        out_specs=(vmem, vmem),
        name="finish",
    )(home, back, momentum)


def solution(mesh):
    in_specs = (P("fsdp", None), P("fsdp", None, "tp"), P("fsdp", None, "tp"))
    out_specs = (P("fsdp", None, "tp"), P("fsdp", None, "tp"))
    return jax.shard_map(local, mesh=mesh, in_specs=in_specs, out_specs=out_specs, check_vma=False)
```

```python
import functools
import math

import jax
import jax.numpy as jnp
from jax import lax
from jax.experimental import pallas as pl
from jax.experimental.pallas import tpu as pltpu
from jax.sharding import PartitionSpec as P

NZ = 4
MESH = pl.DeviceIdType.MESH
F32 = jnp.float32
BF16 = jnp.bfloat16


def landed(ref, sem):
    pltpu.make_async_copy(ref, ref, sem).wait()


def step_kernel(
    groups, x_ref, grads_ref, momentum_ref, home, back,
    xt_ref, og_ref, mom_ref, grads_in, momentum_in, xall, ogs, moms, part, sums, mids, kept, gbuf, nbuf,
    full, wide, xs, gram, mix, thin, final, squares,
    x_s, x_r, f_s, f_r, og_s, og_r, mo_s, mo_r, rs_s, rs_r, n_s, n_r, nf_s, nf_r, h_s, h_r, b_s, b_r, loc,
):
    planes = groups // NZ
    fs = lax.axis_index("fsdp")
    t = lax.axis_index("tp")
    p, z = fs // NZ, fs % NZ
    y, xl = p // 2, p % 2
    ny = groups // NZ // 2
    xh, c = t // 2, t % 2
    partner = xh * 2 + (1 - c)
    tok, count, cols = grads_ref.shape
    chunks = ogs.shape[0]
    each = chunks // 2
    rows = xall.shape[0]
    half = rows // 2
    block = rows // planes
    piece = block // NZ
    lanes = cols // 2

    load_grads = pltpu.make_async_copy(grads_ref, grads_in, loc.at[4])
    load_grads.start()
    load_momentum = pltpu.make_async_copy(momentum_ref, momentum_in, loc.at[5])
    load_momentum.start()

    barrier = pltpu.get_barrier_semaphore()

    def greet(f, tp):
        pl.semaphore_signal(barrier, inc=1, device_id=(f, tp), device_id_type=MESH)

    @pl.loop(1, groups)
    def _(d):
        greet((fs + d) % groups, t)

    @pl.loop(0, planes)
    def _(at):
        greet(at * NZ + z, (1 - xh) * 2 + c)

    greet(fs, partner)

    def x_view(slot, side):
        return xall.at[pl.ds(pl.multiple_of(side * half, half), half), pl.ds(pl.multiple_of(slot * tok, tok), tok)]

    def x_copy(d):
        return pltpu.make_async_remote_copy(
            xt_ref.at[pl.ds(pl.multiple_of(c * half, half), half), :], x_view(z, c), x_s.at[d], x_r.at[z],
            device_id=(p * NZ + (z + d) % NZ, t), device_id_type=MESH)

    def x_forward(slot):
        return pltpu.make_async_remote_copy(
            x_view(slot, c), x_view(slot, c), f_s.at[slot], f_r.at[slot],
            device_id=(fs, partner), device_id_type=MESH)

    def og_view(slot, k):
        return ogs.at[k, pl.ds(pl.multiple_of(slot * tok, tok), tok), :]

    def og_copy(d, k):
        to = (z + d) % NZ
        return pltpu.make_async_remote_copy(
            og_ref.at[to * chunks + k], og_view(z, k), og_s.at[k, d], og_r.at[k, z],
            device_id=(p * NZ + to, t), device_id_type=MESH)

    def mom_copy(d, h):
        to = (z + d) % NZ
        return pltpu.make_async_remote_copy(
            mom_ref.at[pl.ds(to * chunks + h * each, each)], moms.at[z, pl.ds(h * each, each)], mo_s.at[h, d],
            mo_r.at[h, z], device_id=(p * NZ + to, t), device_id_type=MESH)

    def places():
        for m in range(count):
            for h in range(2):
                yield m, h, m // each * chunks + h * each + m % each

    xt_ref[...] = x_ref[...].T
    pl.semaphore_wait(barrier, groups + planes)
    for d in (2, 1, 3):
        x_copy(d).start()

    load_grads.wait()

    @pl.loop(0, tok, step=16)
    def _(at):
        here = pl.ds(pl.multiple_of(at, 16), 16)
        turned = jnp.swapaxes(grads_in[here].astype(F32), 0, 1).astype(BF16)
        for m, h, to in places():
            og_ref[to, here, :] = turned[m, :, h * lanes:(h + 1) * lanes]

    def send_grads(low, high):
        @pl.loop(low, high)
        def _(k):
            for d in (2, 1, 3):
                og_copy(d, k).start()

    send_grads(0, 2)
    load_momentum.wait()
    turned = jnp.swapaxes(momentum_in[...], 0, 1).astype(BF16)
    for m, h, to in places():
        mom_ref[to] = turned[m, :, h * lanes:(h + 1) * lanes]
    for d in (2, 1, 3):
        mom_copy(d, 0).start()
    send_grads(2, chunks)
    for d in (2, 1, 3):
        mom_copy(d, 1).start()

    own_x = pltpu.make_async_copy(xt_ref, xall.at[:, pl.ds(pl.multiple_of(z * tok, tok), tok)], loc.at[0])
    own_og = pltpu.make_async_copy(
        og_ref.at[pl.ds(z * chunks, chunks)], ogs.at[:, pl.ds(pl.multiple_of(z * tok, tok), tok), :], loc.at[1])
    own_mom = pltpu.make_async_copy(mom_ref.at[pl.ds(z * chunks, chunks)], moms.at[z], loc.at[2])
    own_x.start()
    own_og.start()
    own_mom.start()

    for d in (1, 3, 2):
        slot = (z + d) % NZ
        landed(x_view(slot, c), x_r.at[slot])
        x_forward(slot).start()
    own_x.wait()
    own_og.wait()
    own_mom.wait()
    for d in (1, 3, 2):
        slot = (z + d) % NZ
        landed(x_view(slot, 1 - c), f_r.at[slot])

    def across_x(k, source, target):
        return pltpu.make_async_remote_copy(
            source, target, rs_s.at[k, 0], rs_r.at[k, ny],
            device_id=((y * 2 + 1 - xl) * NZ + z, t), device_id_type=MESH)

    def across_y(k, d, source, target):
        return pltpu.make_async_remote_copy(
            source, target, rs_s.at[k, d], rs_r.at[k, y],
            device_id=(((y + d) % ny * 2 + xl) * NZ + z, t), device_id_type=MESH)

    def x_then_y_first(k):
        return across_x(k, part.at[k, 1 - xl], sums.at[k, pl.ds(0, ny)])

    def x_then_y_second(k, d):
        return across_y(k, d, mids.at[k, (y + d) % ny], sums.at[k, ny + y])

    def y_then_x_first(k, d):
        return across_y(k, d, part.at[k, :, (y + d) % ny], sums.at[k, pl.ds(2 * y, 2)])

    def y_then_x_second(k):
        return across_x(k, mids.at[k, 0], sums.at[k, 2 * y])

    def half_view(at, other, side, h):
        return full.at[
            pl.ds(pl.multiple_of(at * block, block), block),
            pl.ds(pl.multiple_of(h * half + side * cols + other * lanes, lanes), lanes)]

    def n_copy(k, other):
        h, m = k // each, k % each
        return pltpu.make_async_remote_copy(
            nbuf.at[k], half_view(p, xh, c, h), n_s.at[k, other], n_r.at[h, p, xh],
            device_id=(m * NZ + z, other * 2 + c), device_id_type=MESH)

    def n_local(k):
        h = k // each
        return pltpu.make_async_copy(nbuf.at[k], half_view(p, xh, c, h), n_r.at[h, p, xh])

    def n_mine(k, other):
        return jnp.logical_and(k % each == p, xh == other)

    def multiply(k):
        for d in range(1, NZ):
            slot = (z + d) % NZ
            landed(og_view(slot, k), og_r.at[k, slot])
        step = 2 * block
        for r in range(ny):
            acc = jnp.dot(xall[r * step:(r + 1) * step, :], ogs[k], preferred_element_type=F32)
            part[k, 0, r] = acc[:block].astype(BF16)
            part[k, 1, r] = acc[block:].astype(BF16)

    def middle_x(k):
        landed(sums.at[k, pl.ds(0, ny)], rs_r.at[k, ny])
        for d in (2, 1, 3, 0):
            to = (y + d) % ny
            total = part[k, xl, to].astype(F32) + sums[k, to].astype(F32)
            if d:
                mids[k, to] = total.astype(BF16)
                x_then_y_second(k, d).start()
            else:
                kept[k] = total

    def middle_y(k):
        mine = part[k, xl, y].astype(F32)
        other = part[k, 1 - xl, y].astype(F32)
        for d in range(1, ny):
            source = (y + d) % ny
            landed(sums.at[k, pl.ds(2 * source, 2)], rs_r.at[k, source])
            mine = mine + sums[k, 2 * source + xl].astype(F32)
            other = other + sums[k, 2 * source + 1 - xl].astype(F32)
        mids[k, 0] = other.astype(BF16)
        y_then_x_second(k).start()
        kept[k] = mine

    def combine_x(k):
        total = kept[k]
        for d in range(1, ny):
            source = (y + d) % ny
            landed(sums.at[k, ny + source], rs_r.at[k, source])
            total = total + sums[k, ny + source].astype(F32)
        combine(k, total)

    def combine_y(k):
        landed(sums.at[k, 2 * y], rs_r.at[k, ny])
        combine(k, kept[k] + sums[k, 2 * y].astype(F32))

    def mom_landed(h):
        for d in range(1, NZ):
            slot = (z + d) % NZ
            landed(moms.at[slot, pl.ds(h * each, each)], mo_r.at[h, slot])

    def combine(k, total):
        momentum = moms[:, k].reshape(block, lanes).astype(F32)
        gbuf[k] = total.astype(BF16)
        nbuf[k] = (total + 0.95 * (0.95 * momentum + total)).astype(BF16)
        for other in range(2):
            mine = n_mine(k, other)

            @pl.when(jnp.logical_not(mine))
            def _():
                n_copy(k, other).start()

            @pl.when(mine)
            def _():
                n_local(k).start()

    def n_forward(h, at, other):
        view = half_view(at, other, c, h)
        return pltpu.make_async_remote_copy(
            view, view, nf_s.at[h, at, other], nf_r.at[h, at, other],
            device_id=(fs, partner), device_id_type=MESH)

    def forward_half(h):
        @pl.loop(0, planes)
        def _(step):
            at = (p + step) % planes
            for other in range(2):
                landed(half_view(at, other, c, h), n_r.at[h, at, other])
                n_forward(h, at, other).start()

    def take_half(h):
        @pl.loop(0, planes)
        def _(step):
            at = (p + step) % planes
            for other in range(2):
                landed(half_view(at, other, 1 - c, h), nf_r.at[h, at, other])

    matrix = z * each + p
    tile = 256
    homes = tile // piece

    def back_copy(to):
        return pltpu.make_async_remote_copy(
            final.at[pl.ds(pl.multiple_of(to * piece, piece), piece), :], back.at[matrix], b_s.at[to],
            b_r.at[matrix], device_id=(to, t), device_id_type=MESH)

    def outer(ref, here, span):
        return lax.dot_general(
            ref[here, span], ref[:, span], (((1,), (1,)), ((), ())), preferred_element_type=F32)

    def square_sum(low, high):
        acc = jnp.zeros((tile, high - low), F32)
        for r in range(0, rows, tile):
            value = full[r:r + tile, low:high].astype(F32)
            acc = acc + value * value
        return jnp.sum(acc)

    def tiles(body):
        @pl.loop(0, rows, step=tile)
        def _(r):
            body(pl.ds(pl.multiple_of(r, tile), tile))

    def first_half():
        def body(here):
            wide[here, :] = outer(full, here, slice(0, half))

        tiles(body)
        squares[0] = square_sum(0, half)

    def mixers():
        def body(here):
            square = jnp.dot(gram[here, :], gram[...], preferred_element_type=F32)
            mix[here, :] = (-4.775 * gram[here, :].astype(F32) + 2.0315 * square).astype(BF16)

        tiles(body)

    def second_half():
        own = pl.ds(pl.multiple_of(half + c * cols, cols), cols)
        rest = pl.ds(pl.multiple_of(half + (1 - c) * cols, cols), cols)

        def with_own(here):
            wide[here, :] = wide[here, :] + outer(full, here, own)

        tiles(with_own)
        take_half(1)
        inverse = 1.0 / (jnp.sqrt(squares[0] + square_sum(half, rows)) + 1e-07)

        def with_rest(here):
            gram[here, :] = ((wide[here, :] + outer(full, here, rest)) * inverse * inverse).astype(BF16)

        tiles(with_rest)
        mixers()

        def advance(here):
            product = jnp.dot(mix[here, :], full[...], preferred_element_type=F32)
            xs[here, :] = ((3.4445 * full[here, :].astype(F32) + product) * inverse).astype(BF16)

        tiles(advance)

        def again(here):
            gram[here, :] = outer(xs, here, slice(None)).astype(BF16)

        tiles(again)
        mixers()
        for h in range(2):
            thin[:, h * lanes:(h + 1) * lanes] = xs[:, pl.ds(
                pl.multiple_of(h * half + c * cols + xh * lanes, lanes), lanes)]

        @pl.loop(0, rows // tile)
        def _(i):
            at = (i + p) % (rows // tile)
            here = pl.ds(pl.multiple_of(at * tile, tile), tile)
            product = jnp.dot(mix[here, :], thin[...], preferred_element_type=F32)
            final[here, :] = (3.4445 * thin[here, :].astype(F32) + product).astype(BF16)

            @pl.loop(0, homes)
            def _(step):
                to = at * homes + (step + z) % homes

                @pl.when(to != fs)
                def _():
                    back_copy(to).start()

        pltpu.make_async_copy(
            final.at[pl.ds(pl.multiple_of(fs * piece, piece), piece), :], back.at[matrix], b_r.at[matrix]).start()

    def home_copy(d):
        to = (z + d) % NZ
        return pltpu.make_async_remote_copy(
            gbuf.at[:, pl.ds(pl.multiple_of(to * piece, piece), piece), :], home.at[pl.ds(z * chunks, chunks)],
            h_s.at[d], h_r.at[z], device_id=(p * NZ + to, t), device_id_type=MESH)

    owner = p < each

    @pl.loop(0, each)
    def _(j):
        k = 2 * j
        multiply(k)
        x_then_y_first(k).start()

        @pl.when(j >= 1)
        def _():
            middle_x(k - 2)

        @pl.when(j == 2)
        def _():
            mom_landed(0)

        late = jnp.logical_and(j >= 2, j < 2 + each // 2)

        @pl.when(late)
        def _():
            combine_x(k - 4)

        multiply(k + 1)
        for d in (2, 1, 3):
            y_then_x_first(k + 1, d).start()

        @pl.when(j >= 1)
        def _():
            middle_y(k - 1)

        @pl.when(late)
        def _():
            combine_y(k - 3)

    middle_x(chunks - 2)

    @pl.when(owner)
    def _():
        forward_half(0)
        take_half(0)
        first_half()

    middle_y(chunks - 1)
    mom_landed(1)

    @pl.loop(each // 2, each)
    def _(j):
        combine_x(2 * j)
        combine_y(2 * j + 1)

    for d in range(1, NZ):
        home_copy(d).start()
    own_home = pltpu.make_async_copy(
        gbuf.at[:, pl.ds(pl.multiple_of(z * piece, piece), piece), :], home.at[pl.ds(z * chunks, chunks)], loc.at[3])
    own_home.start()

    @pl.when(owner)
    def _():
        forward_half(1)
        second_half()

    own_home.wait()
    for d in range(1, NZ):
        slot = (z + d) % NZ
        landed(home.at[pl.ds(slot * chunks, chunks)], h_r.at[slot])

    @pl.loop(0, groups)
    def _(source):
        sp, sz = source // NZ, source % NZ

        @pl.when(sp < each)
        def _():
            landed(back.at[sz * each + sp], b_r.at[sz * each + sp])

    @pl.when(owner)
    def _():
        for h in range(2):
            @pl.loop(0, planes)
            def _(at):
                for other in range(2):
                    n_forward(h, at, other).wait_send()

        @pl.loop(1, groups)
        def _(d):
            back_copy((fs + d) % groups).wait_send()

    for d in range(1, NZ):
        x_copy(d).wait_send()
        x_forward((z + d) % NZ).wait_send()
        home_copy(d).wait_send()
        for h in range(2):
            mom_copy(d, h).wait_send()

    @pl.loop(0, each)
    def _(j):
        x_then_y_first(2 * j).wait_send()
        y_then_x_second(2 * j + 1).wait_send()
        for d in range(1, ny):
            x_then_y_second(2 * j, d).wait_send()
            y_then_x_first(2 * j + 1, d).wait_send()

    @pl.loop(0, chunks)
    def _(k):
        for d in range(1, NZ):
            og_copy(d, k).wait_send()
        for other in range(2):
            @pl.when(jnp.logical_not(n_mine(k, other)))
            def _():
                n_copy(k, other).wait_send()


def finish_kernel(each, rows, home, back, momentum_ref, new_ref, update_ref):
    count, piece, cols = back.shape
    lanes = cols // 2
    for base in range(0, count, 8):
        group = slice(base, base + 8)
        update_ref[:, group, :] = jnp.swapaxes(back[group].astype(F32), 0, 1) * (0.2 * math.sqrt(rows))
        for h in range(2):
            here = slice(h * lanes, (h + 1) * lanes)
            grads = jnp.stack([home[m // each * 2 * each + h * each + m % each] for m in range(base, base + 8)])
            new_ref[:, group, here] = 0.95 * momentum_ref[:, group, here] + jnp.swapaxes(grads.astype(F32), 0, 1)


def local(inputs, out_grads, momentum):
    groups = lax.axis_size("fsdp")
    planes = groups // NZ
    tok, count, cols = out_grads.shape
    rows = inputs.shape[1]
    piece = momentum.shape[0]
    each = count // NZ
    chunks = 2 * each
    lanes = cols // 2
    block = rows // planes
    dma = pltpu.SemaphoreType.DMA
    vmem = pl.BlockSpec(memory_space=pltpu.VMEM)
    hbm = pl.BlockSpec(memory_space=pl.ANY)
    home, back = pl.pallas_call(
        functools.partial(step_kernel, groups),
        out_shape=(
            jax.ShapeDtypeStruct((2 * count, piece, lanes), BF16), jax.ShapeDtypeStruct((count, piece, cols), BF16)),
        in_specs=[vmem, hbm, hbm],
        out_specs=(hbm, hbm),
        scratch_shapes=[
            pltpu.VMEM((rows, tok), BF16),
            pltpu.VMEM((2 * count, tok, lanes), BF16),
            pltpu.VMEM((2 * count, piece, lanes), BF16),
            pltpu.VMEM((tok, count, cols), BF16),
            pltpu.VMEM((piece, count, cols), F32),
            pltpu.VMEM((rows, NZ * tok), BF16),
            pltpu.VMEM((chunks, NZ * tok, lanes), BF16),
            pltpu.VMEM((NZ, chunks, piece, lanes), BF16),
            pltpu.VMEM((chunks, 2, planes // 2, block, lanes), BF16),
            pltpu.VMEM((chunks, planes, block, lanes), BF16),
            pltpu.VMEM((chunks, planes // 2, block, lanes), BF16),
            pltpu.VMEM((chunks, block, lanes), F32),
            pltpu.VMEM((chunks, block, lanes), BF16),
            pltpu.VMEM((chunks, block, lanes), BF16),
            pltpu.VMEM((rows, rows), BF16),
            pltpu.VMEM((rows, rows), F32),
            pltpu.VMEM((rows, rows), BF16),
            pltpu.VMEM((rows, rows), BF16),
            pltpu.VMEM((rows, rows), BF16),
            pltpu.VMEM((rows, cols), BF16),
            pltpu.VMEM((rows, cols), BF16),
            pltpu.SMEM((1,), F32),
            dma((NZ,)), dma((NZ,)), dma((NZ,)), dma((NZ,)),
            dma((chunks, NZ)), dma((chunks, NZ)), dma((2, NZ)), dma((2, NZ)),
            dma((chunks, planes // 2)), dma((chunks, planes // 2 + 1)),
            dma((chunks, 2)), dma((2, planes, 2)), dma((2, planes, 2)), dma((2, planes, 2)),
            dma((NZ,)), dma((NZ,)), dma((groups,)), dma((count,)), dma((6,)),
        ],
        compiler_params=pltpu.CompilerParams(
            collective_id=0, has_side_effects=True, vmem_limit_bytes=60 * 1024 * 1024),
        name="muon_step",
    )(inputs, out_grads, momentum)
    return pl.pallas_call(
        functools.partial(finish_kernel, each, rows),
        out_shape=(jax.ShapeDtypeStruct(momentum.shape, F32), jax.ShapeDtypeStruct(momentum.shape, F32)),
        in_specs=[vmem, vmem, vmem],
        out_specs=(vmem, vmem),
        name="finish",
    )(home, back, momentum)


def solution(mesh):
    in_specs = (P("fsdp", None), P("fsdp", None, "tp"), P("fsdp", None, "tp"))
    out_specs = (P("fsdp", None, "tp"), P("fsdp", None, "tp"))
    return jax.shard_map(local, mesh=mesh, in_specs=in_specs, out_specs=out_specs, check_vma=False)
```
